512 devices in a mesh: rec: 128 (over y, z, core), grp: 4 (over x).
Axes of the slice: x: 4, y: 8, z: 8, core: 2. Of those that a mesh axis runs over, the one named last changes fastest.
Arguments:
- conv_in: bfloat16 [4, 131072, 512], P('grp', 'rec'), may hold values from -6 to 6
- conv5_weight: bfloat16 [1536, 512], P(None, 'grp'), may hold values from -0.15625 to 0.15625
- conv6_weight: bfloat16 [1024, 512], P(None, 'grp'), may hold values from -0.1875 to 0.1875
- conv7_weight: bfloat16 [1024, 512], P(None, 'grp'), may hold values from -0.1875 to 0.1875
- norm_gain: float32 [512], replicated, may hold values from 0.1 to 1.9
- norm_bias: float32 [512], replicated, may hold values from -3 to 3
- proj_weight: bfloat16 [512, 768], P(None, 'grp'), may hold values from -0.25 to 0.25
- proj_bias: float32 [768], replicated, may hold values from -3 to 3
- rec_length: int32 [4], P('grp'), may hold values from 8192 to 16384, as said below
- assign: int32 [3, 4, 16384], P(None, 'grp', 'rec'), may hold values from 0 to 999, as said below
- centroid_init: float32 [1024, 768], P('rec'), may hold values from -6 to 6
- prior_count: float32 [1024], P('rec'), may hold values from 50 to 500
Outputs:
- distortion: float32 [3, 4, 16384], P(None, 'grp', 'rec')
- centroids: float32 [1024, 768], P('rec')
The draws below stay inside these ranges and needn't reach their ends.
Inputs may be any that keep to these rules, and one draw needn't show every extreme that they name: `rec_length`: some recording has all 16384 frames. `assign`: clusters form blocks of 8 consecutive ids (block b holds ids b * 8 to b * 8 + 7). In each iteration the 128 frames of one device name clusters of one block at most 2 times, and in each iteration some block is named exactly 2 times by the frames of every device of one recording.
All inputs are finite; a program needn't handle non-finite values.
Results may differ from the reference program's by a relative error of at most 0.0013.
Values may be sent and summed in bfloat16 or wider, within the bound.
A program may use at most 64 MiB of HBM per device.

```python
import math
import jax
import jax.numpy as jnp
from jax import lax

C = 512
D = 768
K = 1000
FR_DEV = 128
ITERS = 3
RECS = 4
NFR = 16384
TIN = 131072
KL = 8
KPAD = 1024
NOWN = 125
CAP = 2


def draw_rec_length(key, part):
    first_key, second_key = jax.random.split(key)
    lengths = jax.random.randint(first_key, (RECS,), NFR // 2, NFR + 1)
    full_index = jax.random.randint(second_key, (), 0, RECS)
    lengths = jnp.where(jnp.arange(RECS) == full_index, NFR, lengths)
    return lengths.astype(jnp.int32)


def draw_assign(key, part):
    blocks_per_rec = NFR // FR_DEV
    slot_total = NOWN * CAP
    full_key, rest_key = jax.random.split(jax.random.fold_in(key, 17))
    full_owner = jax.random.randint(full_key, (ITERS * RECS,), 0, NOWN)

    def one_block(index):
        block_key = jax.random.fold_in(rest_key, index)
        order_key, shuffle_key, inner_key = jax.random.split(block_key, 3)
        favoured = full_owner[index // blocks_per_rec]
        order = jax.random.permutation(order_key, slot_total).astype(jnp.int32)
        slot_ids = jnp.arange(slot_total, dtype=jnp.int32)
        score = order + jnp.where(slot_ids // CAP == favoured, -slot_total, 0)
        taken = jnp.argsort(score, stable=True)[:FR_DEV]
        owner_id = (taken // CAP).astype(jnp.int32)
        owner_id = owner_id[jax.random.permutation(shuffle_key, FR_DEV)]
        block_size = jnp.minimum(KL, K - owner_id * KL)
        inner_id = jax.random.randint(inner_key, (FR_DEV,), 0, 1 << 20) % block_size
        return (owner_id * KL + inner_id).astype(jnp.int32)
    flat = jax.vmap(one_block)(jnp.arange(ITERS * RECS * blocks_per_rec))
    return flat.reshape(ITERS, RECS, NFR)


def steps_of(stream_key, extent, cuts, least, high):
    def one(dim, shards_of):
        heights = jax.random.uniform(jax.random.fold_in(jax.random.fold_in(stream_key, 6), dim), (shards_of,), jnp.float32, least / len(cuts), high / len(cuts))
        return jnp.repeat(jnp.exp(heights), extent[dim] // shards_of).reshape((-1,) + (1,) * (len(extent) - dim - 1))

    gain = one(*cuts[0])
    for cut in cuts[1:]:
        gain = gain * one(*cut)
    return gain


def normal_values(stream_key, dims, scale, limit, cuts=(), held_as=jnp.bfloat16):
    drawn = jax.random.normal(stream_key, dims, jnp.float32) * scale
    if len(cuts) > 0:
        drawn = steps_of(stream_key, dims, cuts, -0.22, 0.18) * drawn
    return jnp.clip(drawn, min=-limit, max=limit).astype(held_as)


def setup_inputs(seed: int = 0) -> dict:
    splits = jax.random.split(jax.random.key(seed), 13)
    conv_in = normal_values(splits[0], (RECS, TIN, C), 1.0, 6.0, ((0, 4), (1, 128)))
    conv5_weight = normal_values(splits[1], (3 * C, C), (3 * C) ** -0.5, 0.15625, ((1, 4),))
    conv6_weight = normal_values(splits[2], (2 * C, C), (2 * C) ** -0.5, 0.1875, ((1, 4),))
    conv7_weight = normal_values(splits[3], (2 * C, C), (2 * C) ** -0.5, 0.1875, ((1, 4),))
    norm_gain = jnp.clip(1.0 + 0.18 * jax.random.normal(splits[4], (C,), jnp.float32), 0.1, 1.9)
    norm_bias = normal_values(splits[5], (C,), 0.5, 3.0, (), jnp.float32)
    proj_weight = normal_values(splits[6], (C, D), C ** -0.5, 0.25, ((1, 4),))
    proj_bias = normal_values(splits[7], (D,), 0.5, 3.0, (), jnp.float32)
    rec_length = draw_rec_length(jax.random.fold_in(splits[12], 71), 0)
    assign = draw_assign(jax.random.fold_in(splits[12], 71), 0)
    centroid_init = normal_values(splits[10], (KPAD, D), 1.0, 6.0, ((0, 128),), jnp.float32)
    prior_count = jnp.clip(jnp.exp(math.log(500.0) - 2.3025851 * jax.random.uniform(splits[11], (KPAD,), jnp.float32) ** steps_of(splits[11], (KPAD,), ((0, 128),), -0.2, 0.2)), 50.0, 500.0)
    return dict(conv_in=conv_in, conv5_weight=conv5_weight, conv6_weight=conv6_weight, conv7_weight=conv7_weight, norm_gain=norm_gain, norm_bias=norm_bias, proj_weight=proj_weight, proj_bias=proj_bias, rec_length=rec_length, assign=assign, centroid_init=centroid_init, prior_count=prior_count)


def reference(conv_in, conv5_weight, conv6_weight, conv7_weight, norm_gain, norm_bias, proj_weight, proj_bias, rec_length, assign, centroid_init, prior_count):

    def conv_layer(inputs, weight):
        product = jnp.dot(inputs, weight, preferred_element_type=jnp.float32)
        return jax.nn.gelu(product, approximate=False).astype(jnp.bfloat16)

    def encode(signal):
        sample_rows = signal.shape[0]
        channels = signal.shape[1]
        extended = jnp.concatenate([signal, jnp.zeros((1, channels), signal.dtype)], 0)
        stacked = jnp.concatenate([extended[0:sample_rows:2], extended[1:sample_rows:2], extended[2:sample_rows + 1:2]], 1)
        hidden = conv_layer(stacked, conv5_weight)
        hidden = conv_layer(hidden.reshape(-1, 2 * channels), conv6_weight)
        hidden = conv_layer(hidden.reshape(-1, 2 * channels), conv7_weight)
        hidden_wide = hidden.astype(jnp.float32)
        average = lax.optimization_barrier(jnp.mean(hidden_wide, axis=-1, keepdims=True))
        variance = lax.optimization_barrier(jnp.mean((hidden_wide - average) ** 2, axis=-1, keepdims=True))
        normed = ((hidden_wide - average) * lax.rsqrt(variance + 1e-05) * norm_gain + norm_bias).astype(jnp.bfloat16)
        return (jnp.dot(normed, proj_weight, preferred_element_type=jnp.float32) + proj_bias).astype(jnp.bfloat16)
    frames = lax.map(encode, conv_in)
    position = jnp.arange(NFR, dtype=jnp.int32)
    weighting = (position[None, :] < rec_length[:, None]).astype(jnp.float32).reshape(-1)
    frames_wide = frames.astype(jnp.float32).reshape(-1, D)
    centroid = centroid_init
    counts = prior_count
    results = []
    for iteration in range(ITERS):
        chosen = assign[iteration].reshape(-1).astype(jnp.int32)
        coded = centroid.astype(jnp.bfloat16)
        picked = jnp.take(coded, chosen, axis=0).astype(jnp.float32)
        gap_value = frames_wide - picked
        results.append((lax.optimization_barrier(jnp.sum(gap_value * gap_value, axis=1)) / D).reshape(RECS, NFR))
        summed = jax.ops.segment_sum(frames_wide * weighting[:, None], chosen, num_segments=KPAD)
        hit_count = jax.ops.segment_sum(weighting, chosen, num_segments=KPAD)
        updated = counts + hit_count
        centroid = (counts[:, None] * centroid + summed) / updated[:, None]
        counts = updated
    return (jnp.stack(results, 0), centroid)
```

```python
import jax
import jax.numpy as jnp
from jax import lax
from jax.experimental import pallas as pl
from jax.experimental.pallas import tpu as pltpu
from jax.sharding import PartitionSpec as P

ITERS = 3
CAP = 2
MESH = pl.DeviceIdType.MESH


def shifted(value, axis, steps):
    count = lax.axis_size(axis)
    initial, last = (max(0, -steps), min(count, count - steps))
    return lax.ppermute(value, axis, [(source, source + steps) for source in range(initial, last)])


def gather_kernel(*refs):
    ins, outs = refs[:4], refs[4:8]
    send, near, cross = refs[8:]
    rec, grp = lax.axis_index("rec"), lax.axis_index("grp")
    core = lax.rem(rec, 2)
    mate = (rec + 1 - 2 * core, grp)
    right = (rec, lax.rem(grp + 1, 4))
    left = (rec, lax.rem(grp + 3, 4))

    barrier = pltpu.get_barrier_semaphore()
    for peer in (left, right, mate):
        pl.semaphore_signal(barrier, inc=1, device_id=peer, device_id_type=MESH)
    pl.semaphore_wait(barrier, 3)

    def rows(w, half, part):
        quarter = ins[w].shape[0] // 4
        return pl.ds(pl.multiple_of((2 * half + part) * quarter, quarter), quarter)

    def place(w, owner, half, part):
        if outs[w].ndim == 3:
            return outs[w].at[owner, rows(w, half, part), :]
        width = ins[w].shape[1]
        return outs[w].at[rows(w, half, part), pl.ds(pl.multiple_of(owner * width, width), width)]

    started = []

    def copy(w, source, target, slot, arrival, peer):
        made = pltpu.make_async_remote_copy(
            src_ref=source, dst_ref=target, send_sem=send.at[w, slot], recv_sem=arrival.at[w, slot % 6],
            device_id=peer, device_id_type=MESH,
        )
        return made

    owner_of = [lax.rem(grp + 3, 4), lax.rem(grp + 3, 4), lax.rem(grp + 1, 4), lax.rem(grp + 1, 4),
                lax.rem(grp + 2, 4), lax.rem(grp + 2, 4)]
    part_of = [0, 1, 1, 0, 0, 1]
    direct = {}
    for w in range(4):
        for slot, peer in ((0, right), (2, left), (1, right), (3, left)):
            part = part_of[slot]
            made = copy(w, ins[w].at[rows(w, core, part), :], place(w, grp, core, part), slot, near, peer)
            made.start()
            direct[w, slot] = made
    for w in range(4):
        if outs[w].ndim == 3:
            outs[w][grp] = ins[w][...]
        else:
            width = ins[w].shape[1]
            outs[w][:, pl.ds(pl.multiple_of(grp * width, width), width)] = ins[w][...]
    relayed, crossed = {}, {}

    def pass_on(w, slot):
        block = place(w, owner_of[slot], core, part_of[slot])
        if slot in (0, 2):
            hop = copy(w, block, block, 4 + slot // 2, near, right if slot == 0 else left)
            hop.start()
            relayed[w, 4 + slot // 2] = hop
        over = copy(w, block, block, 6 + slot, cross, mate)
        over.start()
        crossed[w, slot] = over

    for w in range(4):
        for slot in (0, 2, 1, 3):
            direct[w, slot].wait_recv()
            pass_on(w, slot)
    for w in range(4):
        for slot in (4, 5):
            relayed[w, slot].wait_recv()
            pass_on(w, slot)
    for w in range(4):
        for slot in range(6):
            crossed[w, slot].wait_recv()
            crossed[w, slot].wait_send()
        for made in [direct[w, slot] for slot in range(4)] + [relayed[w, slot] for slot in (4, 5)]:
            made.wait_send()


def gather_weights(w5, w6, w7, wp):
    shapes = [jax.ShapeDtypeStruct((w.shape[0], 4 * w.shape[1]), w.dtype) for w in (w5, w6, w7)]
    shapes.append(jax.ShapeDtypeStruct((4,) + wp.shape, wp.dtype))
    vmem = pl.BlockSpec(memory_space=pltpu.VMEM)
    return pl.pallas_call(
        gather_kernel,
        out_shape=shapes,
        in_specs=[vmem] * 4,
        out_specs=[vmem] * 4,
        scratch_shapes=[
            pltpu.SemaphoreType.DMA((4, 12)),
            pltpu.SemaphoreType.DMA((4, 6)),
            pltpu.SemaphoreType.DMA((4, 6)),
        ],
        compiler_params=pltpu.CompilerParams(
            collective_id=0, has_side_effects=True, vmem_limit_bytes=32 * 1024 * 1024
        ),
    )(w5, w6, w7, wp)


def total_kernel(part_ref, out_ref, held, send, arrive):
    rec, grp = lax.axis_index("rec"), lax.axis_index("grp")
    barrier = pltpu.get_barrier_semaphore()
    for step in (1, 2, 3):
        pl.semaphore_signal(
            barrier, inc=1, device_id=(rec, lax.rem(grp + step, 4)), device_id_type=MESH
        )
    pl.semaphore_wait(barrier, 3)
    copies = []
    for step in (2, 1, 3):
        made = pltpu.make_async_remote_copy(
            src_ref=part_ref, dst_ref=held.at[grp], send_sem=send.at[step - 1],
            recv_sem=arrive.at[step - 1], device_id=(rec, lax.rem(grp + step, 4)), device_id_type=MESH,
        )
        made.start()
        copies.append(made)
    held[grp] = part_ref[...]
    for made in copies:
        made.wait()
    out_ref[...] = (held[0] + held[1]) + (held[2] + held[3])


def grp_total(part):
    vmem = pl.BlockSpec(memory_space=pltpu.VMEM)
    return pl.pallas_call(
        total_kernel,
        out_shape=jax.ShapeDtypeStruct(part.shape, part.dtype),
        in_specs=[vmem],
        out_specs=vmem,
        scratch_shapes=[
            pltpu.VMEM((4,) + part.shape, part.dtype),
            pltpu.SemaphoreType.DMA((3,)),
            pltpu.SemaphoreType.DMA((3,)),
        ],
        compiler_params=pltpu.CompilerParams(collective_id=1, has_side_effects=True),
    )(part)


def linear(inputs, weight):
    return jnp.dot(inputs, weight, preferred_element_type=jnp.float32)


def conv_layer(inputs, weight):
    return jax.nn.gelu(linear(inputs, weight), approximate=False).astype(jnp.bfloat16)


def shards(
    conv_in,
    conv5_weight,
    conv6_weight,
    conv7_weight,
    norm_gain,
    norm_bias,
    proj_weight,
    proj_bias,
    rec_length,
    assign,
    centroid_init,
    prior_count,
):
    w5, w6, w7, wp = gather_weights(conv5_weight, conv6_weight, conv7_weight, proj_weight)
    signal = conv_in[0]
    sample_rows, channels = signal.shape
    next_row = shifted(signal[:1], "rec", -1)
    paired = signal.reshape(sample_rows // 2, 2 * channels)
    trailing = jnp.concatenate([signal[2::2], next_row], 0)
    stacked = jnp.concatenate([paired, trailing], 1)
    hidden = conv_layer(stacked, w5)
    hidden = conv_layer(hidden.reshape(-1, 2 * channels), w6)
    hidden = conv_layer(hidden.reshape(-1, 2 * channels), w7)
    hidden_wide = hidden.astype(jnp.float32)
    average = jnp.mean(hidden_wide, axis=-1, keepdims=True)
    variance = jnp.mean((hidden_wide - average) ** 2, axis=-1, keepdims=True)
    normed = ((hidden_wide - average) * lax.rsqrt(variance + 1e-05) * norm_gain + norm_bias).astype(
        jnp.bfloat16
    )
    projected = jnp.concatenate([linear(normed, wp[g]) for g in range(4)], 1)
    frames = (projected + proj_bias).astype(jnp.bfloat16)
    frame_count, width = frames.shape

    ranks = lax.axis_size("rec")
    slice_rows = centroid_init.shape[0]
    position = lax.axis_index("rec") * frame_count + jnp.arange(frame_count, dtype=jnp.int32)
    is_live = (position < rec_length[0]).astype(jnp.int32)
    frame_index = jnp.arange(frame_count, dtype=jnp.int32)
    earlier = frame_index[None, :] < frame_index[:, None]
    owner_ids = jnp.arange(ranks, dtype=jnp.int32)
    cluster_ids = jnp.arange(slice_rows, dtype=jnp.int32)

    chosen = assign[:, 0]
    owner = chosen // slice_rows
    inner = chosen - owner * slice_rows
    same = owner[:, :, None] == owner[:, None, :]
    slot = jnp.sum((same & earlier[None]).astype(jnp.int32), axis=2)
    tag = (inner + 1) * (2 * is_live - 1)[None, :]
    picks, rows, tags = [], [], []
    for t in range(ITERS):
        for s in range(CAP):
            pick = (owner[t][None, :] == owner_ids[:, None]) & (slot[t] == s)[None, :]
            picks.append(pick)
            rows.append(linear(pick.astype(jnp.bfloat16), frames).astype(jnp.bfloat16))
            tags.append(jnp.sum(jnp.where(pick, tag[t][None, :], 0), axis=1))
    meta = jnp.stack(tags, 1).astype(jnp.bfloat16)
    meta = jnp.pad(meta, ((0, 0), (0, 128 - meta.shape[1])))
    sent = jnp.concatenate(rows + [meta], 1)
    got = lax.all_to_all(sent, "rec", split_axis=0, concat_axis=0, tiled=True)
    got_tag = got[:, ITERS * CAP * width : ITERS * CAP * width + ITERS * CAP].astype(jnp.int32)

    sums, hits, named = [], [], []
    for t in range(ITERS):
        total, count = 0.0, 0.0
        for s in range(CAP):
            j = t * CAP + s
            block = got[:, j * width : (j + 1) * width]
            live = got_tag[:, j][:, None] == cluster_ids[None, :] + 1
            named.append(live | (got_tag[:, j][:, None] == -cluster_ids[None, :] - 1))
            total = total + linear(live.astype(jnp.bfloat16).T, block)
            count = count + jnp.sum(live.astype(jnp.float32), axis=0)
        sums.append(total)
        hits.append(count)
    sums, hits = jnp.concatenate(sums, 0), jnp.concatenate(hits, 0)
    part = jnp.concatenate([sums, jnp.broadcast_to(hits[:, None], (hits.shape[0], 128))], 1)
    part = grp_total(part)
    centroid, counts = centroid_init, prior_count
    back = []
    for t in range(ITERS):
        coded = centroid.astype(jnp.bfloat16)
        for s in range(CAP):
            j = t * CAP + s
            block = got[:, j * width : (j + 1) * width].astype(jnp.float32)
            gap = block - linear(named[j].astype(jnp.bfloat16), coded)
            back.append(jnp.sum(gap * gap, axis=1) / width)
        lot = part[t * slice_rows : (t + 1) * slice_rows]
        updated = counts + lot[:, width]
        centroid = (counts[:, None] * centroid + lot[:, :width]) / updated[:, None]
        counts = updated
    back = jnp.pad(jnp.stack(back, 1), ((0, 0), (0, 128 - ITERS * CAP)))
    back = lax.all_to_all(back, "rec", split_axis=0, concat_axis=0, tiled=True)
    results = []
    for t in range(ITERS):
        one = 0.0
        for s in range(CAP):
            j = t * CAP + s
            one = one + jnp.sum(jnp.where(picks[j], back[:, j][:, None], 0.0), axis=0)
        results.append(one)
    return (jnp.stack(results, 0)[:, None, :], centroid)


def solution(mesh):
    in_specs = (
        P("grp", "rec", None),
        P(None, "grp"),
        P(None, "grp"),
        P(None, "grp"),
        P(),
        P(),
        P(None, "grp"),
        P(),
        P("grp"),
        P(None, "grp", "rec"),
        P("rec", None),
        P("rec"),
    )
    out_specs = (P(None, "grp", "rec"), P("rec", None))
    return jax.shard_map(shards, mesh=mesh, in_specs=in_specs, out_specs=out_specs, check_vma=False)
```

```python
import jax
import jax.numpy as jnp
from jax import lax
from jax.experimental import pallas as pl
from jax.experimental.pallas import tpu as pltpu
from jax.sharding import PartitionSpec as P

ITERS = 3
CAP = 2
MESH = pl.DeviceIdType.MESH


def shifted(value, axis, steps):
    count = lax.axis_size(axis)
    initial, last = (max(0, -steps), min(count, count - steps))
    return lax.ppermute(value, axis, [(source, source + steps) for source in range(initial, last)])


def gather_kernel(*refs):
    ins, outs = refs[:4], refs[4:8]
    send, near, cross = refs[8:]
    rec, grp = lax.axis_index("rec"), lax.axis_index("grp")
    core = lax.rem(rec, 2)
    mate = (rec + 1 - 2 * core, grp)
    right = (rec, lax.rem(grp + 1, 4))
    left = (rec, lax.rem(grp + 3, 4))

    barrier = pltpu.get_barrier_semaphore()
    for peer in (left, right, mate):
        pl.semaphore_signal(barrier, inc=1, device_id=peer, device_id_type=MESH)
    pl.semaphore_wait(barrier, 3)

    def rows(w, half, part):
        quarter = ins[w].shape[0] // 4
        return pl.ds(pl.multiple_of((2 * half + part) * quarter, quarter), quarter)

    def place(w, owner, half, part):
        if outs[w].ndim == 3:
            return outs[w].at[owner, rows(w, half, part), :]
        width = ins[w].shape[1]
        return outs[w].at[rows(w, half, part), pl.ds(pl.multiple_of(owner * width, width), width)]

    started = []

    def copy(w, source, target, slot, arrival, peer):
        made = pltpu.make_async_remote_copy(
            src_ref=source, dst_ref=target, send_sem=send.at[w, slot], recv_sem=arrival.at[w, slot % 6],
            device_id=peer, device_id_type=MESH,
        )
        return made

    owner_of = [lax.rem(grp + 3, 4), lax.rem(grp + 3, 4), lax.rem(grp + 1, 4), lax.rem(grp + 1, 4),
                lax.rem(grp + 2, 4), lax.rem(grp + 2, 4)]
    part_of = [0, 1, 1, 0, 0, 1]
    direct = {}
    for w in range(4):
        for slot, peer in ((0, right), (2, left), (1, right), (3, left)):
            part = part_of[slot]
            made = copy(w, ins[w].at[rows(w, core, part), :], place(w, grp, core, part), slot, near, peer)
            made.start()
            direct[w, slot] = made
    for w in range(4):
        if outs[w].ndim == 3:
            outs[w][grp] = ins[w][...]
        else:
            width = ins[w].shape[1]
            outs[w][:, pl.ds(pl.multiple_of(grp * width, width), width)] = ins[w][...]
    relayed, crossed = {}, {}

    def pass_on(w, slot):
        block = place(w, owner_of[slot], core, part_of[slot])
        if slot in (0, 2):
            hop = copy(w, block, block, 4 + slot // 2, near, right if slot == 0 else left)
            hop.start()
            relayed[w, 4 + slot // 2] = hop
        over = copy(w, block, block, 6 + slot, cross, mate)
        over.start()
        crossed[w, slot] = over

    for w in range(4):
        for slot in (0, 2, 1, 3):
            direct[w, slot].wait_recv()
            pass_on(w, slot)
    for w in range(4):
        for slot in (4, 5):
            relayed[w, slot].wait_recv()
            pass_on(w, slot)
    for w in range(4):
        for slot in range(6):
            crossed[w, slot].wait_recv()
            crossed[w, slot].wait_send()
        for made in [direct[w, slot] for slot in range(4)] + [relayed[w, slot] for slot in (4, 5)]:
            made.wait_send()


def gather_weights(w5, w6, w7, wp):
    shapes = [jax.ShapeDtypeStruct((w.shape[0], 4 * w.shape[1]), w.dtype) for w in (w5, w6, w7)]
    shapes.append(jax.ShapeDtypeStruct((4,) + wp.shape, wp.dtype))
    vmem = pl.BlockSpec(memory_space=pltpu.VMEM)
    return pl.pallas_call(
        gather_kernel,
        out_shape=shapes,
        in_specs=[vmem] * 4,
        out_specs=[vmem] * 4,
        scratch_shapes=[
            pltpu.SemaphoreType.DMA((4, 12)),
            pltpu.SemaphoreType.DMA((4, 6)),
            pltpu.SemaphoreType.DMA((4, 6)),
        ],
        compiler_params=pltpu.CompilerParams(
            collective_id=0, has_side_effects=True, vmem_limit_bytes=32 * 1024 * 1024
        ),
    )(w5, w6, w7, wp)


PIECES = 40


def refresh_kernel(
    sent, start_ref, prior_ref, back_out, centroid_out,
    got, onehot, part, held, code, reply, back,
    go_sem, come_sem, own_sem, part_send, part_come, reply_send, reply_come,
):
    rec, grp = lax.axis_index("rec"), lax.axis_index("grp")
    ranks = sent.shape[0]
    lot = ranks // 8
    width = start_ref.shape[1]
    lanes = width // 6

    def peer_of(k):
        shift = lax.rem(k * 53, ranks)
        y = lax.rem(rec // 16 + shift // 16, ranks // 16)
        z = lax.rem(lax.rem(rec // 2, 8) + lax.rem(shift // 2, 8), 8)
        core = lax.rem(rec + shift, 2)
        return (y * 8 + z) * 2 + core

    barrier = pltpu.get_barrier_semaphore()

    @pl.loop(1, ranks)
    def _(k):
        pl.semaphore_signal(barrier, inc=1, device_id=(peer_of(k), grp), device_id_type=MESH)

    for step in (1, 2, 3):
        pl.semaphore_signal(
            barrier, inc=1, device_id=(rec, lax.rem(grp + step, 4)), device_id_type=MESH
        )
    pl.semaphore_wait(barrier, ranks + 2)

    @pl.loop(1, ranks)
    def _(k):
        peer = peer_of(k)
        pltpu.make_async_remote_copy(
            src_ref=sent.at[peer], dst_ref=got.at[rec], send_sem=go_sem, recv_sem=come_sem,
            device_id=(peer, grp), device_id_type=MESH,
        ).start()

    own = pltpu.make_async_copy(sent.at[rec], got.at[rec], own_sem)
    own.start()
    own.wait()
    every = pltpu.make_async_remote_copy(
        src_ref=sent.at[pl.ds(0, ranks - 1)], dst_ref=got.at[pl.ds(0, ranks - 1)], send_sem=go_sem,
        recv_sem=come_sem, device_id=(peer_of(1), grp), device_id_type=MESH,
    )
    every.wait_recv()

    shape = (lot, PIECES, 128)
    piece = lax.broadcasted_iota(jnp.int32, shape, 1)
    lane = lax.broadcasted_iota(jnp.int32, shape, 2)
    in_row = lane == piece // 6
    column = (lot, PIECES, 1)
    piece_column = lax.broadcasted_iota(jnp.int32, column, 1)
    base = ((piece_column // 12) * 6 + lax.rem(piece_column, 6)) * 8 - 1
    wide_lane = lax.broadcasted_iota(jnp.int32, (lot, PIECES, 256), 2)
    contract = (((0,), (0,)), ((), ()))
    ones = jnp.ones((lot * PIECES, 128), jnp.bfloat16)

    def add_up(c, carry):
        sums, hits = carry
        block = got[pl.ds(c * lot, lot)].astype(jnp.float32)
        meta = jnp.broadcast_to(block[:, 36:37, :], shape)
        tag = jnp.sum(jnp.where(in_row, meta, 0.0), axis=2, keepdims=True).astype(jnp.int32)
        spot = jnp.where(tag == 0, -1, base + jnp.abs(tag))
        hot = jnp.where(wide_lane == spot, 1.0, 0.0)
        live = jnp.where(tag > 0, hot, 0.0)
        onehot[pl.ds(pl.multiple_of(c * lot * PIECES, lot * PIECES), lot * PIECES), :] = (
            hot.reshape(lot * PIECES, 256).astype(jnp.bfloat16)
        )
        live = live.reshape(lot * PIECES, 256).astype(jnp.bfloat16)
        flat = block.reshape(lot * PIECES, 128).astype(jnp.bfloat16)
        sums = sums + lax.dot_general(live, flat, contract, preferred_element_type=jnp.float32)
        hits = hits + lax.dot_general(live, ones, contract, preferred_element_type=jnp.float32)
        return sums, hits

    zero = jnp.zeros((256, 128), jnp.float32)
    sums, hits = lax.fori_loop(0, 8, add_up, (zero, zero))
    part[0:144, :] = sums[0:144]
    for t in range(ITERS):
        part[144 + 8 * t : 152 + 8 * t, :] = hits[48 * t : 48 * t + 8]

    copies = []
    for step in (2, 1, 3):
        made = pltpu.make_async_remote_copy(
            src_ref=part, dst_ref=held.at[grp], send_sem=part_send.at[step - 1],
            recv_sem=part_come.at[step - 1], device_id=(rec, lax.rem(grp + step, 4)), device_id_type=MESH,
        )
        made.start()
        copies.append(made)
    held[grp] = part[...]
    for made in copies:
        made.wait()

    code[144:256, :] = jnp.zeros((112, 128), jnp.float32)
    for l in range(6):
        centroid = start_ref[:, l * lanes : (l + 1) * lanes]
        counts = prior_ref[...]
        for t in range(ITERS):
            at = (t * 6 + l) * 8
            code[at : at + 8, :] = centroid.astype(jnp.bfloat16).astype(jnp.float32)
            total = (held[0, at : at + 8] + held[1, at : at + 8]) + (
                held[2, at : at + 8] + held[3, at : at + 8]
            )
            at = 144 + 8 * t
            more = (held[0, at : at + 8] + held[1, at : at + 8]) + (
                held[2, at : at + 8] + held[3, at : at + 8]
            )
            updated = counts + more
            centroid = (counts * centroid + total) / updated
            counts = updated
        centroid_out[:, l * lanes : (l + 1) * lanes] = centroid
    table = code[...].astype(jnp.bfloat16)

    @pl.loop(0, 8)
    def _(c):
        block = got[pl.ds(c * lot, lot)].astype(jnp.float32)
        hot = onehot[pl.ds(pl.multiple_of(c * lot * PIECES, lot * PIECES), lot * PIECES), :]
        named = jnp.dot(hot, table, preferred_element_type=jnp.float32).reshape(shape)
        gap = block - named
        apart = jnp.sum(gap * gap, axis=2, keepdims=True)
        spread = jnp.where(in_row, apart, 0.0)
        reply[pl.ds(c * lot, lot)] = jnp.sum(spread, axis=1, keepdims=True) / width

    @pl.loop(1, ranks)
    def _(k):
        peer = peer_of(k)
        pltpu.make_async_remote_copy(
            src_ref=reply.at[peer], dst_ref=back.at[rec], send_sem=reply_send, recv_sem=reply_come,
            device_id=(peer, grp), device_id_type=MESH,
        ).start()

    own = pltpu.make_async_copy(reply.at[rec], back.at[rec], own_sem)
    own.start()
    own.wait()
    all_back = pltpu.make_async_remote_copy(
        src_ref=reply.at[pl.ds(0, ranks - 1)], dst_ref=back.at[pl.ds(0, ranks - 1)], send_sem=reply_send,
        recv_sem=reply_come, device_id=(peer_of(1), grp), device_id_type=MESH,
    )
    all_back.wait_recv()
    back_out[...] = back[...]
    every.wait_send()
    all_back.wait_send()


def refresh(sent, start, prior):
    ranks = sent.shape[0]
    vmem = pl.BlockSpec(memory_space=pltpu.VMEM)
    return pl.pallas_call(
        refresh_kernel,
        out_shape=[
            jax.ShapeDtypeStruct((ranks, 1, 128), jnp.float32),
            jax.ShapeDtypeStruct(start.shape, jnp.float32),
        ],
        in_specs=[vmem] * 3,
        out_specs=[vmem] * 2,
        scratch_shapes=[
            pltpu.VMEM((ranks, PIECES, 128), jnp.bfloat16),
            pltpu.VMEM((ranks * PIECES, 256), jnp.bfloat16),
            pltpu.VMEM((168, 128), jnp.float32),
            pltpu.VMEM((4, 168, 128), jnp.float32),
            pltpu.VMEM((256, 128), jnp.float32),
            pltpu.VMEM((ranks, 1, 128), jnp.float32),
            pltpu.VMEM((ranks, 1, 128), jnp.float32),
            pltpu.SemaphoreType.DMA,
            pltpu.SemaphoreType.DMA,
            pltpu.SemaphoreType.DMA,
            pltpu.SemaphoreType.DMA((3,)),
            pltpu.SemaphoreType.DMA((3,)),
            pltpu.SemaphoreType.DMA,
            pltpu.SemaphoreType.DMA,
        ],
        compiler_params=pltpu.CompilerParams(
            collective_id=1, has_side_effects=True, vmem_limit_bytes=32 * 1024 * 1024
        ),
    )(sent, start, prior)


def linear(inputs, weight):
    return jnp.dot(inputs, weight, preferred_element_type=jnp.float32)


def conv_layer(inputs, weight):
    return jax.nn.gelu(linear(inputs, weight), approximate=False).astype(jnp.bfloat16)


def shards(
    conv_in,
    conv5_weight,
    conv6_weight,
    conv7_weight,
    norm_gain,
    norm_bias,
    proj_weight,
    proj_bias,
    rec_length,
    assign,
    centroid_init,
    prior_count,
):
    w5, w6, w7, wp = gather_weights(conv5_weight, conv6_weight, conv7_weight, proj_weight)
    signal = conv_in[0]
    sample_rows, channels = signal.shape
    next_row = shifted(signal[:1], "rec", -1)
    paired = signal.reshape(sample_rows // 2, 2 * channels)
    trailing = jnp.concatenate([signal[2::2], next_row], 0)
    stacked = jnp.concatenate([paired, trailing], 1)
    hidden = conv_layer(stacked, w5)
    hidden = conv_layer(hidden.reshape(-1, 2 * channels), w6)
    hidden = conv_layer(hidden.reshape(-1, 2 * channels), w7)
    hidden_wide = hidden.astype(jnp.float32)
    average = jnp.mean(hidden_wide, axis=-1, keepdims=True)
    variance = jnp.mean((hidden_wide - average) ** 2, axis=-1, keepdims=True)
    normed = ((hidden_wide - average) * lax.rsqrt(variance + 1e-05) * norm_gain + norm_bias).astype(
        jnp.bfloat16
    )
    projected = jnp.concatenate([linear(normed, wp[g]) for g in range(4)], 1)
    frames = (projected + proj_bias).astype(jnp.bfloat16)
    frame_count, width = frames.shape

    ranks = lax.axis_size("rec")
    slice_rows = centroid_init.shape[0]
    position = lax.axis_index("rec") * frame_count + jnp.arange(frame_count, dtype=jnp.int32)
    is_live = (position < rec_length[0]).astype(jnp.int32)
    frame_index = jnp.arange(frame_count, dtype=jnp.int32)
    earlier = frame_index[None, :] < frame_index[:, None]
    owner_ids = jnp.arange(ranks, dtype=jnp.int32)

    chosen = assign[:, 0]
    owner = chosen // slice_rows
    inner = chosen - owner * slice_rows
    same = owner[:, :, None] == owner[:, None, :]
    slot = jnp.sum((same & earlier[None]).astype(jnp.int32), axis=2)
    tag = (inner + 1) * (2 * is_live - 1)[None, :]
    picks, rows, tags = [], [], []
    for t in range(ITERS):
        for s in range(CAP):
            pick = (owner[t][None, :] == owner_ids[:, None]) & (slot[t] == s)[None, :]
            picks.append(pick)
            rows.append(linear(pick.astype(jnp.bfloat16), frames).astype(jnp.bfloat16))
            tags.append(jnp.sum(jnp.where(pick, tag[t][None, :], 0), axis=1))
    meta = jnp.stack(tags, 1).astype(jnp.bfloat16)
    meta = jnp.pad(meta, ((0, 0), (0, PIECES * 128 - 6 * width - meta.shape[1])))
    sent = jnp.concatenate(rows + [meta], 1).reshape(ranks, PIECES, 128)
    prior = jnp.broadcast_to(prior_count[:, None], (slice_rows, 128))
    back, centroid = refresh(sent, centroid_init, prior)
    back = back[:, 0]
    results = []
    for t in range(ITERS):
        one = 0.0
        for s in range(CAP):
            j = t * CAP + s
            one = one + jnp.sum(jnp.where(picks[j], back[:, j][:, None], 0.0), axis=0)
        results.append(one)
    return (jnp.stack(results, 0)[:, None, :], centroid)


def solution(mesh):
    in_specs = (
        P("grp", "rec", None),
        P(None, "grp"),
        P(None, "grp"),
        P(None, "grp"),
        P(),
        P(),
        P(None, "grp"),
        P(),
        P("grp"),
        P(None, "grp", "rec"),
        P("rec", None),
        P("rec"),
    )
    out_specs = (P(None, "grp", "rec"), P("rec", None))
    return jax.shard_map(shards, mesh=mesh, in_specs=in_specs, out_specs=out_specs, check_vma=False)
```

```python
import jax
import jax.numpy as jnp
from jax import lax
from jax.experimental import pallas as pl
from jax.experimental.pallas import tpu as pltpu
from jax.sharding import PartitionSpec as P

ITERS = 3
CAP = 2
PIECES = 40
MESH = pl.DeviceIdType.MESH


def whole_kernel(
    x_ref, a5, a6, a7, ap, gain_ref, shift_ref, bias_ref, length_ref, assign_ref, start_ref, prior_ref,
    dist_out, centroid_out,
    o5, o6, o7, op, halo, xf, h5, h6, fr, picked, laid, sent,
    got, onehot, part, held, code, reply, back,
    send, near, cross, halo_send, halo_come,
    go_sem, come_sem, own_sem, part_send, part_come, reply_send, reply_come,
):
    ins, outs = (a5, a6, a7, ap), (o5, o6, o7, op)
    rec, grp = lax.axis_index("rec"), lax.axis_index("grp")
    core = lax.rem(rec, 2)
    mate = (rec + 1 - 2 * core, grp)
    right = (rec, lax.rem(grp + 1, 4))
    left = (rec, lax.rem(grp + 3, 4))
    ranks = sent.shape[0]
    lot = ranks // 8
    width = start_ref.shape[1]
    lanes = width // 6
    steps = x_ref.shape[0]
    frames = steps // 8

    def peer_of(k):
        shift = lax.rem(k * 53, ranks)
        y = lax.rem(rec // 16 + shift // 16, ranks // 16)
        z = lax.rem(lax.rem(rec // 2, 8) + lax.rem(shift // 2, 8), 8)
        across = lax.rem(rec + shift, 2)
        return (y * 8 + z) * 2 + across

    barrier = pltpu.get_barrier_semaphore()
    for step in (1, 2, 3):
        pl.semaphore_signal(
            barrier, inc=1, device_id=(rec, lax.rem(grp + step, 4)), device_id_type=MESH
        )

    @pl.loop(1, ranks)
    def _(k):
        pl.semaphore_signal(barrier, inc=1, device_id=(peer_of(k), grp), device_id_type=MESH)

    pl.semaphore_wait(barrier, ranks + 2)

    next_rows = pltpu.make_async_remote_copy(
        src_ref=x_ref.at[pl.ds(0, 16), :], dst_ref=halo, send_sem=halo_send, recv_sem=halo_come,
        device_id=(lax.rem(rec + ranks - 1, ranks), grp), device_id_type=MESH,
    )
    next_rows.start()

    def rows(w, half, part):
        quarter = ins[w].shape[0] // 4
        return pl.ds(pl.multiple_of((2 * half + part) * quarter, quarter), quarter)

    def place(w, owner, half, part):
        if outs[w].ndim == 3:
            return outs[w].at[owner, rows(w, half, part), :]
        width = ins[w].shape[1]
        return outs[w].at[rows(w, half, part), pl.ds(pl.multiple_of(owner * width, width), width)]

    started = []

    def copy(w, source, target, slot, arrival, peer):
        made = pltpu.make_async_remote_copy(
            src_ref=source, dst_ref=target, send_sem=send.at[w, slot], recv_sem=arrival.at[w, slot % 6],
            device_id=peer, device_id_type=MESH,
        )
        return made

    owner_of = [lax.rem(grp + 3, 4), lax.rem(grp + 3, 4), lax.rem(grp + 1, 4), lax.rem(grp + 1, 4),
                lax.rem(grp + 2, 4), lax.rem(grp + 2, 4)]
    part_of = [0, 1, 1, 0, 0, 1]
    direct = {}
    for w in range(4):
        for slot, peer in ((0, right), (2, left), (1, right), (3, left)):
            side = part_of[slot]
            made = copy(w, ins[w].at[rows(w, core, side), :], place(w, grp, core, side), slot, near, peer)
            made.start()
            direct[w, slot] = made
    for w in range(4):
        if outs[w].ndim == 3:
            outs[w][grp] = ins[w][...]
        else:
            wide = ins[w].shape[1]
            outs[w][:, pl.ds(pl.multiple_of(grp * wide, wide), wide)] = ins[w][...]

    square = (ranks, frames)
    blocks = lax.broadcasted_iota(jnp.int32, square, 0)
    frame_row = lax.broadcasted_iota(jnp.int32, (1, frames), 1)
    lane_row = lax.broadcasted_iota(jnp.int32, (ranks, 128), 1)
    earlier = jnp.where(
        lax.broadcasted_iota(jnp.int32, (frames, frames), 0)
        < lax.broadcasted_iota(jnp.int32, (frames, frames), 1), 1.0, 0.0
    ).astype(jnp.bfloat16)
    sign = jnp.where(rec * frames + frame_row < length_ref[0], 1.0, -1.0)
    meta = jnp.zeros((ranks, 128), jnp.float32)
    for t in range(ITERS):
        chosen = assign_ref[t]
        owner = chosen // 8
        tag = (chosen - owner * 8 + 1).astype(jnp.float32) * sign
        hit = blocks == owner
        before = jnp.dot(
            jnp.where(hit, 1.0, 0.0).astype(jnp.bfloat16), earlier, preferred_element_type=jnp.float32
        )
        for s in range(CAP):
            pick = jnp.where(hit, jnp.where(before == s, 1.0, 0.0), 0.0)
            picked[t * CAP + s] = pick
            label = jnp.sum(pick * tag, axis=1, keepdims=True)
            meta = meta + jnp.where(lane_row == t * CAP + s, label, 0.0)
    laid[pl.ds(36, ranks, stride=PIECES), :] = meta
    for q in range(37, PIECES):
        laid[pl.ds(q, ranks, stride=PIECES), :] = jnp.zeros((ranks, 128), jnp.float32)
    for l in range(x_ref.shape[1] // 128):
        xf[l, 0:steps, :] = x_ref[:, l * 128 : (l + 1) * 128].astype(jnp.float32)

    relayed, crossed = {}, {}

    def pass_on(w, slot):
        block = place(w, owner_of[slot], core, part_of[slot])
        if slot in (0, 2):
            hop = copy(w, block, block, 4 + slot // 2, near, right if slot == 0 else left)
            hop.start()
            relayed[w, 4 + slot // 2] = hop
        over = copy(w, block, block, 6 + slot, cross, mate)
        over.start()
        crossed[w, slot] = over

    for w in range(4):
        for slot in (0, 2, 1, 3):
            direct[w, slot].wait_recv()
            pass_on(w, slot)

    def gelu(v):
        return (0.5 * v * (1.0 + lax.erf(v * 0.7071067811865476))).astype(jnp.bfloat16)

    def dot(a, b):
        return jnp.dot(a, b, preferred_element_type=jnp.float32)

    channels = x_ref.shape[1]

    def layer5():
        next_rows.wait_recv()
        last = jnp.where(rec == ranks - 1, 0.0, 1.0)
        store(xf, steps, halo[...].astype(jnp.float32)[0:8] * last)
        for c in range(2):
            base = c * (steps // 2)
            total = jnp.zeros((steps // 4, channels), jnp.float32)
            for tap in range(3):
                rows_in = strided(xf, base + tap, steps // 4)
                total = total + dot(rows_in, o5[tap * channels : (tap + 1) * channels, :])
            store(h5, c * (steps // 4), gelu(total))

    def strided(ref, start, count):
        parts = [ref[l, pl.ds(start, count, stride=2), :] for l in range(channels // 128)]
        return jnp.concatenate(parts, 1).astype(jnp.bfloat16)

    def store(ref, start, value):
        value = value.astype(jnp.float32)
        for l in range(channels // 128):
            ref[l, start : start + value.shape[0], :] = value[:, l * 128 : (l + 1) * 128]

    def layer6():
        count = steps // 4
        store(h6, 0, gelu(dot(strided(h5, 0, count), o6[0:channels, :])
                          + dot(strided(h5, 1, count), o6[channels : 2 * channels, :])))

    def layer7():
        hidden = gelu(dot(strided(h6, 0, frames), o7[0:channels, :])
                      + dot(strided(h6, 1, frames), o7[channels : 2 * channels, :])).astype(jnp.float32)
        average = jnp.mean(hidden, axis=1, keepdims=True)
        away = hidden - average
        variance = jnp.mean(away * away, axis=1, keepdims=True)
        normed = away * lax.rsqrt(variance + 1e-05) * gain_ref[...] + shift_ref[...]
        store(h5, 0, normed)

    def project():
        normed = jnp.concatenate([h5[l, 0:frames, :] for l in range(channels // 128)], 1).astype(jnp.bfloat16)
        pieces = [dot(normed, op[owner]) for owner in range(4)]
        fr[...] = (jnp.concatenate(pieces, 1) + bias_ref[...]).astype(jnp.bfloat16)

    stages = (layer5, layer6, layer7, project)

    def finish(w):
        for slot in range(6):
            crossed[w, slot].wait_recv()
        stages[w]()

    for w in range(4):
        for slot in (4, 5):
            relayed[w, slot].wait_recv()
            pass_on(w, slot)
        if w >= 1:
            finish(w - 1)
    finish(3)
    for j in range(ITERS * CAP):
        rows_out = dot(picked[j].astype(jnp.bfloat16), fr[...])
        for l in range(6):
            laid[pl.ds(j * 6 + l, ranks, stride=PIECES), :] = rows_out[:, l * lanes : (l + 1) * lanes]

    @pl.loop(0, 8)
    def _(c):
        flat = laid[pl.ds(pl.multiple_of(c * lot * PIECES, lot * PIECES), lot * PIECES), :]
        sent[pl.ds(c * lot, lot)] = flat.reshape(lot, PIECES, 128).astype(jnp.bfloat16)

    @pl.loop(1, ranks)
    def _(k):
        peer = peer_of(k)
        pltpu.make_async_remote_copy(
            src_ref=sent.at[peer], dst_ref=got.at[rec], send_sem=go_sem, recv_sem=come_sem,
            device_id=(peer, grp), device_id_type=MESH,
        ).start()

    own = pltpu.make_async_copy(sent.at[rec], got.at[rec], own_sem)
    own.start()
    own.wait()
    every = pltpu.make_async_remote_copy(
        src_ref=sent.at[pl.ds(0, ranks - 1)], dst_ref=got.at[pl.ds(0, ranks - 1)], send_sem=go_sem,
        recv_sem=come_sem, device_id=(peer_of(1), grp), device_id_type=MESH,
    )
    every.wait_recv()

    shape = (lot, PIECES, 128)
    piece = lax.broadcasted_iota(jnp.int32, shape, 1)
    lane = lax.broadcasted_iota(jnp.int32, shape, 2)
    in_row = lane == piece // 6
    column = (lot, PIECES, 1)
    piece_column = lax.broadcasted_iota(jnp.int32, column, 1)
    base = ((piece_column // 12) * 6 + lax.rem(piece_column, 6)) * 8 - 1
    wide_lane = lax.broadcasted_iota(jnp.int32, (lot, PIECES, 256), 2)
    contract = (((0,), (0,)), ((), ()))
    ones = jnp.ones((lot * PIECES, 128), jnp.bfloat16)

    def add_up(c, carry):
        sums, hits = carry
        block = got[pl.ds(c * lot, lot)].astype(jnp.float32)
        meta = jnp.broadcast_to(block[:, 36:37, :], shape)
        tag = jnp.sum(jnp.where(in_row, meta, 0.0), axis=2, keepdims=True).astype(jnp.int32)
        spot = jnp.where(tag == 0, -1, base + jnp.abs(tag))
        hot = jnp.where(wide_lane == spot, 1.0, 0.0)
        live = jnp.where(tag > 0, hot, 0.0)
        onehot[pl.ds(pl.multiple_of(c * lot * PIECES, lot * PIECES), lot * PIECES), :] = (
            hot.reshape(lot * PIECES, 256).astype(jnp.bfloat16)
        )
        live = live.reshape(lot * PIECES, 256).astype(jnp.bfloat16)
        flat = block.reshape(lot * PIECES, 128).astype(jnp.bfloat16)
        sums = sums + lax.dot_general(live, flat, contract, preferred_element_type=jnp.float32)
        hits = hits + lax.dot_general(live, ones, contract, preferred_element_type=jnp.float32)
        return sums, hits

    zero = jnp.zeros((256, 128), jnp.float32)
    sums, hits = lax.fori_loop(0, 8, add_up, (zero, zero))
    part[0:144, :] = sums[0:144]
    for t in range(ITERS):
        part[144 + 8 * t : 152 + 8 * t, :] = hits[48 * t : 48 * t + 8]

    copies = []
    for step in (2, 1, 3):
        made = pltpu.make_async_remote_copy(
            src_ref=part, dst_ref=held.at[grp], send_sem=part_send.at[step - 1],
            recv_sem=part_come.at[step - 1], device_id=(rec, lax.rem(grp + step, 4)), device_id_type=MESH,
        )
        made.start()
        copies.append(made)
    held[grp] = part[...]
    for made in copies:
        made.wait()

    code[144:256, :] = jnp.zeros((112, 128), jnp.float32)
    for l in range(6):
        centroid = start_ref[:, l * lanes : (l + 1) * lanes]
        counts = prior_ref[...]
        for t in range(ITERS):
            at = (t * 6 + l) * 8
            code[at : at + 8, :] = centroid.astype(jnp.bfloat16).astype(jnp.float32)
            total = (held[0, at : at + 8] + held[1, at : at + 8]) + (
                held[2, at : at + 8] + held[3, at : at + 8]
            )
            at = 144 + 8 * t
            more = (held[0, at : at + 8] + held[1, at : at + 8]) + (
                held[2, at : at + 8] + held[3, at : at + 8]
            )
            updated = counts + more
            centroid = (counts * centroid + total) / updated
            counts = updated
        centroid_out[:, l * lanes : (l + 1) * lanes] = centroid
    table = code[...].astype(jnp.bfloat16)

    @pl.loop(0, 8)
    def _(c):
        block = got[pl.ds(c * lot, lot)].astype(jnp.float32)
        hot = onehot[pl.ds(pl.multiple_of(c * lot * PIECES, lot * PIECES), lot * PIECES), :]
        named = jnp.dot(hot, table, preferred_element_type=jnp.float32).reshape(shape)
        gap = block - named
        apart = jnp.sum(gap * gap, axis=2, keepdims=True)
        spread = jnp.where(in_row, apart, 0.0)
        reply[pl.ds(c * lot, lot)] = jnp.sum(spread, axis=1, keepdims=True) / width

    @pl.loop(1, ranks)
    def _(k):
        peer = peer_of(k)
        pltpu.make_async_remote_copy(
            src_ref=reply.at[peer], dst_ref=back.at[rec], send_sem=reply_send, recv_sem=reply_come,
            device_id=(peer, grp), device_id_type=MESH,
        ).start()

    own = pltpu.make_async_copy(reply.at[rec], back.at[rec], own_sem)
    own.start()
    own.wait()
    all_back = pltpu.make_async_remote_copy(
        src_ref=reply.at[pl.ds(0, ranks - 1)], dst_ref=back.at[pl.ds(0, ranks - 1)], send_sem=reply_send,
        recv_sem=reply_come, device_id=(peer_of(1), grp), device_id_type=MESH,
    )
    all_back.wait_recv()
    replies = back[...].reshape(ranks, 128)
    for t in range(ITERS):
        one = jnp.zeros((1, frames), jnp.float32)
        for s in range(CAP):
            j = t * CAP + s
            one = one + jnp.sum(picked[j] * replies[:, j : j + 1], axis=0, keepdims=True)
        dist_out[t] = one
    next_rows.wait_send()
    for w in range(4):
        for slot in range(6):
            crossed[w, slot].wait_send()
        for made in [direct[w, slot] for slot in range(4)] + [relayed[w, slot] for slot in (4, 5)]:
            made.wait_send()
    every.wait_send()
    all_back.wait_send()


def shards(
    conv_in,
    conv5_weight,
    conv6_weight,
    conv7_weight,
    norm_gain,
    norm_bias,
    proj_weight,
    proj_bias,
    rec_length,
    assign,
    centroid_init,
    prior_count,
):
    ranks = lax.axis_size("rec")
    signal = conv_in[0]
    steps, channels = signal.shape
    frames = steps // 8
    slots, width = centroid_init.shape
    prior = jnp.broadcast_to(prior_count[:, None], (slots, 128))
    vmem = pl.BlockSpec(memory_space=pltpu.VMEM)
    smem = pl.BlockSpec(memory_space=pltpu.SMEM)
    bf16, f32, dma = jnp.bfloat16, jnp.float32, pltpu.SemaphoreType.DMA
    return pl.pallas_call(
        whole_kernel,
        out_shape=[
            jax.ShapeDtypeStruct(assign.shape, f32),
            jax.ShapeDtypeStruct(centroid_init.shape, f32),
        ],
        in_specs=[vmem] * 8 + [smem] + [vmem] * 3,
        out_specs=[vmem] * 2,
        scratch_shapes=[
            pltpu.VMEM((3 * channels, channels), bf16),
            pltpu.VMEM((2 * channels, channels), bf16),
            pltpu.VMEM((2 * channels, channels), bf16),
            pltpu.VMEM((4,) + proj_weight.shape, bf16),
            pltpu.VMEM((16, channels), bf16),
            pltpu.VMEM((channels // 128, steps + 8, 128), f32),
            pltpu.VMEM((channels // 128, steps // 2, 128), f32),
            pltpu.VMEM((channels // 128, steps // 4, 128), f32),
            pltpu.VMEM((frames, width), bf16),
            pltpu.VMEM((ITERS * CAP, ranks, frames), f32),
            pltpu.VMEM((ranks * PIECES, 128), f32),
            pltpu.VMEM((ranks, PIECES, 128), bf16),
            pltpu.VMEM((ranks, PIECES, 128), bf16),
            pltpu.VMEM((ranks * PIECES, 256), bf16),
            pltpu.VMEM((168, 128), f32),
            pltpu.VMEM((4, 168, 128), f32),
            pltpu.VMEM((256, 128), f32),
            pltpu.VMEM((ranks, 1, 128), f32),
            pltpu.VMEM((ranks, 1, 128), f32),
            dma((4, 12)), dma((4, 6)), dma((4, 6)), dma, dma,
            dma, dma, dma, dma((3,)), dma((3,)), dma, dma,
        ],
        compiler_params=pltpu.CompilerParams(
            collective_id=0, has_side_effects=True, vmem_limit_bytes=48 * 1024 * 1024
        ),
    )(
        signal, conv5_weight, conv6_weight, conv7_weight, proj_weight, norm_gain[None], norm_bias[None],
        proj_bias[None], rec_length, assign, centroid_init, prior,
    )


def solution(mesh):
    in_specs = (
        P("grp", "rec", None),
        P(None, "grp"),
        P(None, "grp"),
        P(None, "grp"),
        P(),
        P(),
        P(None, "grp"),
        P(),
        P("grp"),
        P(None, "grp", "rec"),
        P("rec", None),
        P("rec"),
    )
    out_specs = (P(None, "grp", "rec"), P("rec", None))
    return jax.shard_map(shards, mesh=mesh, in_specs=in_specs, out_specs=out_specs, check_vma=False)
```

```python
import jax
import jax.numpy as jnp
from jax import lax
from jax.experimental import pallas as pl
from jax.experimental.pallas import tpu as pltpu
from jax.sharding import PartitionSpec as P

ITERS = 3
CAP = 2
PIECES = 40
MESH = pl.DeviceIdType.MESH


def whole_kernel(
    x_ref, a5, a6, a7, ap, gain_ref, shift_ref, bias_ref, length_ref, assign_ref, start_ref, prior_ref,
    dist_out, centroid_out,
    o5, o6, o7, op, halo, xv, xf, h5, h6, fr, picked, laid, sent,
    got, onehot, part, held, code, reply, back,
    send, near, cross, load_sem, halo_send, halo_come,
    go_sem, come_sem, own_sem, part_send, part_come, reply_send, reply_come,
):
    ins, outs = (a5, a6, a7, ap), (o5, o6, o7, op)
    rec, grp = lax.axis_index("rec"), lax.axis_index("grp")
    core = lax.rem(rec, 2)
    mate = (rec + 1 - 2 * core, grp)
    right = (rec, lax.rem(grp + 1, 4))
    left = (rec, lax.rem(grp + 3, 4))
    ranks = sent.shape[0]
    lot = ranks // 8
    width = start_ref.shape[1]
    lanes = width // 6
    steps = x_ref.shape[0]
    frames = steps // 8

    across = (core, 1 - core)
    depth = [lax.rem(lax.div(rec, 2) + dz, 8) * 2 for dz in range(8)]
    level = lax.div(rec, 16)

    def for_peers(act):
        def turn(i, skip):
            for dz in range(8):
                base = lax.rem(level + i + dz, 8) * 16 + depth[dz]
                for dc in range(2):
                    if not (skip and dz == 0 and dc == 0):
                        act(base + across[dc])

        turn(0, True)

        @pl.loop(1, ranks // 16)
        def _(i):
            turn(i, False)

    barrier = pltpu.get_barrier_semaphore()
    for step in (1, 2, 3):
        pl.semaphore_signal(
            barrier, inc=1, device_id=(rec, lax.rem(grp + step, 4)), device_id_type=MESH
        )

    @for_peers
    def _(peer):
        pl.semaphore_signal(barrier, inc=1, device_id=(peer, grp), device_id_type=MESH)

    load = pltpu.make_async_copy(x_ref, xv, load_sem.at[4])
    load.start()

    pl.semaphore_wait(barrier, ranks + 2)

    next_rows = pltpu.make_async_remote_copy(
        src_ref=x_ref.at[pl.ds(0, 16), :], dst_ref=halo, send_sem=halo_send, recv_sem=halo_come,
        device_id=(lax.rem(rec + ranks - 1, ranks), grp), device_id_type=MESH,
    )
    next_rows.start()

    def rows(w, half, part):
        quarter = ins[w].shape[0] // 4
        return pl.ds(pl.multiple_of((2 * half + part) * quarter, quarter), quarter)

    def place(w, owner, half, part):
        if outs[w].ndim == 3:
            return outs[w].at[owner, rows(w, half, part), :]
        width = ins[w].shape[1]
        return outs[w].at[rows(w, half, part), pl.ds(pl.multiple_of(owner * width, width), width)]

    started = []

    def copy(w, source, target, slot, arrival, peer):
        made = pltpu.make_async_remote_copy(
            src_ref=source, dst_ref=target, send_sem=send.at[w, slot], recv_sem=arrival.at[w, slot % 6],
            device_id=peer, device_id_type=MESH,
        )
        return made

    owner_of = [lax.rem(grp + 3, 4), lax.rem(grp + 3, 4), lax.rem(grp + 1, 4), lax.rem(grp + 1, 4),
                lax.rem(grp + 2, 4), lax.rem(grp + 2, 4)]
    part_of = [0, 1, 1, 0, 0, 1]
    direct = {}
    for w in range(4):
        for slot, peer in ((0, right), (2, left), (1, right), (3, left)):
            side = part_of[slot]
            made = copy(w, ins[w].at[rows(w, core, side), :], place(w, grp, core, side), slot, near, peer)
            made.start()
            direct[w, slot] = made
    loads = []
    for w in range(4):
        wide = ins[w].shape[1]
        kept = outs[w].at[grp] if w == 3 else outs[w].at[:, pl.ds(pl.multiple_of(grp * wide, wide), wide)]
        loads.append(pltpu.make_async_copy(ins[w], kept, load_sem.at[w]))
        loads[w].start()

    square = (ranks, frames)
    blocks = lax.broadcasted_iota(jnp.int32, square, 0)
    frame_row = lax.broadcasted_iota(jnp.int32, (1, frames), 1)
    lane_row = lax.broadcasted_iota(jnp.int32, (ranks, 128), 1)
    earlier = jnp.where(
        lax.broadcasted_iota(jnp.int32, (frames, frames), 0)
        < lax.broadcasted_iota(jnp.int32, (frames, frames), 1), 1.0, 0.0
    ).astype(jnp.bfloat16)
    sign = jnp.where(rec * frames + frame_row < length_ref[0], 1.0, -1.0)
    meta = jnp.zeros((ranks, 128), jnp.float32)
    for t in range(ITERS):
        chosen = assign_ref[t]
        owner = chosen // 8
        tag = (chosen - owner * 8 + 1).astype(jnp.float32) * sign
        hit = blocks == owner
        before = jnp.dot(
            jnp.where(hit, 1.0, 0.0).astype(jnp.bfloat16), earlier, preferred_element_type=jnp.float32
        )
        for s in range(CAP):
            pick = jnp.where(hit, jnp.where(before == s, 1.0, 0.0), 0.0)
            picked[t * CAP + s] = pick
            label = jnp.sum(pick * tag, axis=1, keepdims=True)
            meta = meta + jnp.where(lane_row == t * CAP + s, label, 0.0)
    laid[pl.ds(36, ranks, stride=PIECES), :] = meta
    for q in range(37, PIECES):
        laid[pl.ds(q, ranks, stride=PIECES), :] = jnp.zeros((ranks, 128), jnp.float32)
    load.wait()
    for l in range(x_ref.shape[1] // 128):
        xf[l, 0:steps, :] = xv[:, l * 128 : (l + 1) * 128].astype(jnp.float32)

    relayed, crossed = {}, {}

    def pass_on(w, slot):
        block = place(w, owner_of[slot], core, part_of[slot])
        if slot in (0, 2):
            hop = copy(w, block, block, 4 + slot // 2, near, right if slot == 0 else left)
            hop.start()
            relayed[w, 4 + slot // 2] = hop
        over = copy(w, block, block, 6 + slot, cross, mate)
        over.start()
        crossed[w, slot] = over

    for w in range(4):
        for slot in (0, 2, 1, 3):
            direct[w, slot].wait_recv()
            pass_on(w, slot)

    def gelu(v):
        return (0.5 * v * (1.0 + lax.erf(v * 0.7071067811865476))).astype(jnp.bfloat16)

    def dot(a, b):
        return jnp.dot(a, b, preferred_element_type=jnp.float32)

    channels = x_ref.shape[1]

    def layer5():
        next_rows.wait_recv()
        last = jnp.where(rec == ranks - 1, 0.0, 1.0)
        store(xf, steps, halo[...].astype(jnp.float32)[0:8] * last)
        for c in range(2):
            base = c * (steps // 2)
            total = jnp.zeros((steps // 4, channels), jnp.float32)
            for tap in range(3):
                rows_in = strided(xf, base + tap, steps // 4)
                total = total + dot(rows_in, o5[tap * channels : (tap + 1) * channels, :])
            store(h5, c * (steps // 4), gelu(total))

    def strided(ref, start, count):
        parts = [ref[l, pl.ds(start, count, stride=2), :] for l in range(channels // 128)]
        return jnp.concatenate(parts, 1).astype(jnp.bfloat16)

    def store(ref, start, value):
        value = value.astype(jnp.float32)
        for l in range(channels // 128):
            ref[l, start : start + value.shape[0], :] = value[:, l * 128 : (l + 1) * 128]

    def layer6():
        count = steps // 4
        store(h6, 0, gelu(dot(strided(h5, 0, count), o6[0:channels, :])
                          + dot(strided(h5, 1, count), o6[channels : 2 * channels, :])))

    def layer7():
        hidden = gelu(dot(strided(h6, 0, frames), o7[0:channels, :])
                      + dot(strided(h6, 1, frames), o7[channels : 2 * channels, :])).astype(jnp.float32)
        average = jnp.mean(hidden, axis=1, keepdims=True)
        away = hidden - average
        variance = jnp.mean(away * away, axis=1, keepdims=True)
        normed = away * lax.rsqrt(variance + 1e-05) * gain_ref[...] + shift_ref[...]
        store(h5, 0, normed)

    def project():
        normed = jnp.concatenate([h5[l, 0:frames, :] for l in range(channels // 128)], 1).astype(jnp.bfloat16)
        pieces = [
            lax.dot_general(normed, op[owner], (((1,), (1,)), ((), ())), preferred_element_type=jnp.float32)
            for owner in range(4)
        ]
        fr[...] = (jnp.concatenate(pieces, 1) + bias_ref[...]).astype(jnp.bfloat16)

    stages = (layer5, layer6, layer7, project)

    def finish(w):
        for slot in range(6):
            crossed[w, slot].wait_recv()
        loads[w].wait()
        stages[w]()

    for w in range(4):
        for slot in (4, 5):
            relayed[w, slot].wait_recv()
            pass_on(w, slot)
        if w >= 1:
            finish(w - 1)
    finish(3)
    for j in range(ITERS * CAP):
        rows_out = dot(picked[j].astype(jnp.bfloat16), fr[...])
        for l in range(6):
            laid[pl.ds(j * 6 + l, ranks, stride=PIECES), :] = rows_out[:, l * lanes : (l + 1) * lanes]

    @pl.loop(0, 8)
    def _(c):
        flat = laid[pl.ds(pl.multiple_of(c * lot * PIECES, lot * PIECES), lot * PIECES), :]
        sent[pl.ds(c * lot, lot)] = flat.reshape(lot, PIECES, 128).astype(jnp.bfloat16)

    @for_peers
    def _(peer):
        pltpu.make_async_remote_copy(
            src_ref=sent.at[peer], dst_ref=got.at[rec], send_sem=go_sem, recv_sem=come_sem,
            device_id=(peer, grp), device_id_type=MESH,
        ).start()

    own = pltpu.make_async_copy(sent.at[rec], got.at[rec], own_sem)
    own.start()
    own.wait()
    every = pltpu.make_async_remote_copy(
        src_ref=sent.at[pl.ds(0, ranks - 1)], dst_ref=got.at[pl.ds(0, ranks - 1)], send_sem=go_sem,
        recv_sem=come_sem, device_id=mate, device_id_type=MESH,
    )
    every.wait_recv()

    shape = (lot, PIECES, 128)
    piece = lax.broadcasted_iota(jnp.int32, shape, 1)
    lane = lax.broadcasted_iota(jnp.int32, shape, 2)
    in_row = lane == piece // 6
    column = (lot, PIECES, 1)
    piece_column = lax.broadcasted_iota(jnp.int32, column, 1)
    base = ((piece_column // 12) * 6 + lax.rem(piece_column, 6)) * 8 - 1
    wide_lane = lax.broadcasted_iota(jnp.int32, (lot, PIECES, 256), 2)
    contract = (((0,), (0,)), ((), ()))
    ones = jnp.ones((lot * PIECES, 128), jnp.bfloat16)

    def add_up(c, carry):
        sums, hits = carry
        block = got[pl.ds(c * lot, lot)].astype(jnp.float32)
        meta = jnp.broadcast_to(block[:, 36:37, :], shape)
        tag = jnp.sum(jnp.where(in_row, meta, 0.0), axis=2, keepdims=True).astype(jnp.int32)
        spot = jnp.where(tag == 0, -1, base + jnp.abs(tag))
        hot = jnp.where(wide_lane == spot, 1.0, 0.0)
        live = jnp.where(tag > 0, hot, 0.0)
        onehot[pl.ds(pl.multiple_of(c * lot * PIECES, lot * PIECES), lot * PIECES), :] = (
            hot.reshape(lot * PIECES, 256).astype(jnp.bfloat16)
        )
        live = live.reshape(lot * PIECES, 256).astype(jnp.bfloat16)
        flat = block.reshape(lot * PIECES, 128).astype(jnp.bfloat16)
        sums = sums + lax.dot_general(live, flat, contract, preferred_element_type=jnp.float32)
        hits = hits + lax.dot_general(live, ones, contract, preferred_element_type=jnp.float32)
        return sums, hits

    zero = jnp.zeros((256, 128), jnp.float32)
    sums, hits = lax.fori_loop(0, 8, add_up, (zero, zero))
    part[0:144, :] = sums[0:144]
    for t in range(ITERS):
        part[144 + 8 * t : 152 + 8 * t, :] = hits[48 * t : 48 * t + 8]

    copies = []
    for step in (2, 1, 3):
        made = pltpu.make_async_remote_copy(
            src_ref=part, dst_ref=held.at[grp], send_sem=part_send.at[step - 1],
            recv_sem=part_come.at[step - 1], device_id=(rec, lax.rem(grp + step, 4)), device_id_type=MESH,
        )
        made.start()
        copies.append(made)
    held[grp] = part[...]
    for made in copies:
        made.wait()

    code[144:256, :] = jnp.zeros((112, 128), jnp.float32)
    for l in range(6):
        centroid = start_ref[:, l * lanes : (l + 1) * lanes]
        counts = prior_ref[...]
        for t in range(ITERS):
            at = (t * 6 + l) * 8
            code[at : at + 8, :] = centroid.astype(jnp.bfloat16).astype(jnp.float32)
            total = (held[0, at : at + 8] + held[1, at : at + 8]) + (
                held[2, at : at + 8] + held[3, at : at + 8]
            )
            at = 144 + 8 * t
            more = (held[0, at : at + 8] + held[1, at : at + 8]) + (
                held[2, at : at + 8] + held[3, at : at + 8]
            )
            updated = counts + more
            centroid = (counts * centroid + total) / updated
            counts = updated
        centroid_out[:, l * lanes : (l + 1) * lanes] = centroid
    table = code[...].astype(jnp.bfloat16)

    @pl.loop(0, 8)
    def _(c):
        block = got[pl.ds(c * lot, lot)].astype(jnp.float32)
        hot = onehot[pl.ds(pl.multiple_of(c * lot * PIECES, lot * PIECES), lot * PIECES), :]
        named = jnp.dot(hot, table, preferred_element_type=jnp.float32).reshape(shape)
        gap = block - named
        apart = jnp.sum(gap * gap, axis=2, keepdims=True)
        spread = jnp.where(in_row, apart, 0.0)
        reply[pl.ds(c * lot, lot)] = jnp.sum(spread, axis=1, keepdims=True) / width

    @for_peers
    def _(peer):
        pltpu.make_async_remote_copy(
            src_ref=reply.at[peer], dst_ref=back.at[rec], send_sem=reply_send, recv_sem=reply_come,
            device_id=(peer, grp), device_id_type=MESH,
        ).start()

    own = pltpu.make_async_copy(reply.at[rec], back.at[rec], own_sem)
    own.start()
    own.wait()
    all_back = pltpu.make_async_remote_copy(
        src_ref=reply.at[pl.ds(0, ranks - 1)], dst_ref=back.at[pl.ds(0, ranks - 1)], send_sem=reply_send,
        recv_sem=reply_come, device_id=mate, device_id_type=MESH,
    )
    all_back.wait_recv()
    replies = back[...].reshape(ranks, 128)
    for t in range(ITERS):
        one = jnp.zeros((1, frames), jnp.float32)
        for s in range(CAP):
            j = t * CAP + s
            one = one + jnp.sum(picked[j] * replies[:, j : j + 1], axis=0, keepdims=True)
        dist_out[t] = one
    next_rows.wait_send()
    for w in range(4):
        for slot in range(6):
            crossed[w, slot].wait_send()
        for made in [direct[w, slot] for slot in range(4)] + [relayed[w, slot] for slot in (4, 5)]:
            made.wait_send()
    every.wait_send()
    all_back.wait_send()


def shards(
    conv_in,
    conv5_weight,
    conv6_weight,
    conv7_weight,
    norm_gain,
    norm_bias,
    proj_weight,
    proj_bias,
    rec_length,
    assign,
    centroid_init,
    prior_count,
):
    ranks = lax.axis_size("rec")
    signal = conv_in[0]
    steps, channels = signal.shape
    frames = steps // 8
    slots, width = centroid_init.shape
    prior = jnp.broadcast_to(prior_count[:, None], (slots, 128))
    vmem = pl.BlockSpec(memory_space=pltpu.VMEM)
    hbm = pl.BlockSpec(memory_space=pltpu.HBM)
    smem = pl.BlockSpec(memory_space=pltpu.SMEM)
    bf16, f32, dma = jnp.bfloat16, jnp.float32, pltpu.SemaphoreType.DMA
    return pl.pallas_call(
        whole_kernel,
        out_shape=[
            jax.ShapeDtypeStruct(assign.shape, f32),
            jax.ShapeDtypeStruct(centroid_init.shape, f32),
        ],
        in_specs=[hbm] * 5 + [vmem] * 3 + [smem] + [vmem] * 3,
        out_specs=[vmem] * 2,
        scratch_shapes=[
            pltpu.VMEM((3 * channels, channels), bf16),
            pltpu.VMEM((2 * channels, channels), bf16),
            pltpu.VMEM((2 * channels, channels), bf16),
            pltpu.VMEM((4,) + proj_weight.shape[::-1], bf16),
            pltpu.VMEM((16, channels), bf16),
            pltpu.VMEM((steps, channels), bf16),
            pltpu.VMEM((channels // 128, steps + 8, 128), f32),
            pltpu.VMEM((channels // 128, steps // 2, 128), f32),
            pltpu.VMEM((channels // 128, steps // 4, 128), f32),
            pltpu.VMEM((frames, width), bf16),
            pltpu.VMEM((ITERS * CAP, ranks, frames), f32),
            pltpu.VMEM((ranks * PIECES, 128), f32),
            pltpu.VMEM((ranks, PIECES, 128), bf16),
            pltpu.VMEM((ranks, PIECES, 128), bf16),
            pltpu.VMEM((ranks * PIECES, 256), bf16),
            pltpu.VMEM((168, 128), f32),
            pltpu.VMEM((4, 168, 128), f32),
            pltpu.VMEM((256, 128), f32),
            pltpu.VMEM((ranks, 1, 128), f32),
            pltpu.VMEM((ranks, 1, 128), f32),
            dma((4, 12)), dma((4, 6)), dma((4, 6)), dma((5,)), dma, dma,
            dma, dma, dma, dma((3,)), dma((3,)), dma, dma,
        ],
        compiler_params=pltpu.CompilerParams(
            collective_id=0, has_side_effects=True, vmem_limit_bytes=63 * 1024 * 1024
        ),
    )(
        signal, conv5_weight, conv6_weight, conv7_weight, proj_weight.T, norm_gain[None], norm_bias[None],
        proj_bias[None], rec_length, assign, centroid_init, prior,
    )


def solution(mesh):
    in_specs = (
        P("grp", "rec", None),
        P(None, "grp"),
        P(None, "grp"),
        P(None, "grp"),
        P(),
        P(),
        P(None, "grp"),
        P(),
        P("grp"),
        P(None, "grp", "rec"),
        P("rec", None),
        P("rec"),
    )
    out_specs = (P(None, "grp", "rec"), P("rec", None))
    return jax.shard_map(shards, mesh=mesh, in_specs=in_specs, out_specs=out_specs, check_vma=False)
```

```python
import jax
import jax.numpy as jnp
from jax import lax
from jax.experimental import pallas as pl
from jax.experimental.pallas import tpu as pltpu
from jax.sharding import PartitionSpec as P

ITERS = 3
CAP = 2
PIECES = 40
MESH = pl.DeviceIdType.MESH


def whole_kernel(
    x_ref, a5, a6, a7, ap, gain_ref, shift_ref, bias_ref, length_ref, assign_ref, start_ref, prior_ref,
    dist_out, centroid_out,
    o5, o6, o7, op, halo, xv, xf, h5, h6, fr, picked, laid, sent,
    got, onehot, part, held, code, reply, back,
    send, near, cross, load_sem, halo_send, halo_come,
    go_sem, come_sem, own_sem, part_send, part_come, reply_send, reply_come,
):
    ins, outs = (a5, a6, a7, ap), (o5, o6, o7, op)
    rec, grp = lax.axis_index("rec"), lax.axis_index("grp")
    core = lax.rem(rec, 2)
    mate = (rec + 1 - 2 * core, grp)
    right = (rec, lax.rem(grp + 1, 4))
    left = (rec, lax.rem(grp + 3, 4))
    ranks = sent.shape[0]
    lot = ranks // 8
    width = start_ref.shape[1]
    lanes = width // 6
    steps = x_ref.shape[0]
    frames = steps // 8

    across = (core, 1 - core)
    depth = [lax.rem(lax.div(rec, 2) + dz, 8) * 2 for dz in range(8)]
    level = lax.div(rec, 16)

    def for_peers(act):
        def turn(i, skip):
            for dz in range(8):
                base = lax.rem(level + i + dz, 8) * 16 + depth[dz]
                for dc in range(2):
                    if not (skip and dz == 0 and dc == 0):
                        act(base + across[dc])

        turn(0, True)

        @pl.loop(1, ranks // 16)
        def _(i):
            turn(i, False)

    barrier = pltpu.get_barrier_semaphore()
    for step in (1, 2, 3):
        pl.semaphore_signal(
            barrier, inc=1, device_id=(rec, lax.rem(grp + step, 4)), device_id_type=MESH
        )

    @for_peers
    def _(peer):
        pl.semaphore_signal(barrier, inc=1, device_id=(peer, grp), device_id_type=MESH)

    load = pltpu.make_async_copy(x_ref, xv, load_sem.at[4])
    load.start()

    pl.semaphore_wait(barrier, ranks + 2)

    next_rows = pltpu.make_async_remote_copy(
        src_ref=x_ref.at[pl.ds(0, 16), :], dst_ref=halo, send_sem=halo_send, recv_sem=halo_come,
        device_id=(lax.rem(rec + ranks - 1, ranks), grp), device_id_type=MESH,
    )
    next_rows.start()

    def rows(w, half, part):
        quarter = ins[w].shape[0] // 4
        return pl.ds(pl.multiple_of((2 * half + part) * quarter, quarter), quarter)

    def place(w, owner, half, part):
        if outs[w].ndim == 3:
            return outs[w].at[owner, rows(w, half, part), :]
        width = ins[w].shape[1]
        return outs[w].at[rows(w, half, part), pl.ds(pl.multiple_of(owner * width, width), width)]

    started = []

    def copy(w, source, target, slot, arrival, peer):
        made = pltpu.make_async_remote_copy(
            src_ref=source, dst_ref=target, send_sem=send.at[w, slot], recv_sem=arrival.at[w, slot % 6],
            device_id=peer, device_id_type=MESH,
        )
        return made

    owner_of = [lax.rem(grp + 3, 4), lax.rem(grp + 3, 4), lax.rem(grp + 1, 4), lax.rem(grp + 1, 4),
                lax.rem(grp + 2, 4), lax.rem(grp + 2, 4)]
    part_of = [0, 1, 1, 0, 0, 1]
    direct = {}
    for w in range(4):
        for slot, peer in ((0, right), (2, left), (1, right), (3, left)):
            side = part_of[slot]
            made = copy(w, ins[w].at[rows(w, core, side), :], place(w, grp, core, side), slot, near, peer)
            made.start()
            direct[w, slot] = made
    loads = []
    for w in range(4):
        wide = ins[w].shape[1]
        kept = outs[w].at[grp] if w == 3 else outs[w].at[:, pl.ds(pl.multiple_of(grp * wide, wide), wide)]
        loads.append(pltpu.make_async_copy(ins[w], kept, load_sem.at[w]))
        loads[w].start()

    square = (ranks, frames)
    blocks = lax.broadcasted_iota(jnp.int32, square, 0)
    frame_row = lax.broadcasted_iota(jnp.int32, (1, frames), 1)
    lane_row = lax.broadcasted_iota(jnp.int32, (ranks, 128), 1)
    earlier = jnp.where(
        lax.broadcasted_iota(jnp.int32, (frames, frames), 0)
        < lax.broadcasted_iota(jnp.int32, (frames, frames), 1), 1.0, 0.0
    ).astype(jnp.bfloat16)
    sign = jnp.where(rec * frames + frame_row < length_ref[0], 1.0, -1.0)
    meta = jnp.zeros((ranks, 128), jnp.float32)
    for t in range(ITERS):
        chosen = assign_ref[t]
        owner = chosen // 8
        tag = (chosen - owner * 8 + 1).astype(jnp.float32) * sign
        hit = blocks == owner
        before = jnp.dot(
            jnp.where(hit, 1.0, 0.0).astype(jnp.bfloat16), earlier, preferred_element_type=jnp.float32
        )
        for s in range(CAP):
            pick = jnp.where(hit, jnp.where(before == s, 1.0, 0.0), 0.0)
            picked[t * CAP + s] = pick
            label = jnp.sum(pick * tag, axis=1, keepdims=True)
            meta = meta + jnp.where(lane_row == t * CAP + s, label, 0.0)
    laid[pl.ds(36, ranks, stride=PIECES), :] = meta
    for q in range(37, PIECES):
        laid[pl.ds(q, ranks, stride=PIECES), :] = jnp.zeros((ranks, 128), jnp.float32)
    load.wait()
    for l in range(x_ref.shape[1] // 128):
        xf[l, 0:steps, :] = xv[:, l * 128 : (l + 1) * 128].astype(jnp.float32)

    relayed, crossed = {}, {}

    def pass_on(w, slot):
        block = place(w, owner_of[slot], core, part_of[slot])
        if slot in (0, 2):
            hop = copy(w, block, block, 4 + slot // 2, near, right if slot == 0 else left)
            hop.start()
            relayed[w, 4 + slot // 2] = hop
        over = copy(w, block, block, 6 + slot, cross, mate)
        over.start()
        crossed[w, slot] = over

    for w in range(4):
        for slot in (0, 2, 1, 3):
            direct[w, slot].wait_recv()
            pass_on(w, slot)

    def gelu(v):
        return (0.5 * v * (1.0 + lax.erf(v * 0.7071067811865476))).astype(jnp.bfloat16)

    def dot(a, b):
        return jnp.dot(a, b, preferred_element_type=jnp.float32)

    channels = x_ref.shape[1]

    def layer5():
        next_rows.wait_recv()
        last = jnp.where(rec == ranks - 1, 0.0, 1.0)
        store(xf, steps, halo[...].astype(jnp.float32)[0:8] * last)
        for c in range(2):
            base = c * (steps // 2)
            total = jnp.zeros((steps // 4, channels), jnp.float32)
            for tap in range(3):
                rows_in = strided(xf, base + tap, steps // 4)
                total = total + dot(rows_in, o5[tap * channels : (tap + 1) * channels, :])
            store(h5, c * (steps // 4), gelu(total))

    def strided(ref, start, count):
        parts = [ref[l, pl.ds(start, count, stride=2), :] for l in range(channels // 128)]
        return jnp.concatenate(parts, 1).astype(jnp.bfloat16)

    def store(ref, start, value):
        value = value.astype(jnp.float32)
        for l in range(channels // 128):
            ref[l, start : start + value.shape[0], :] = value[:, l * 128 : (l + 1) * 128]

    def layer6():
        count = steps // 4
        store(h6, 0, gelu(dot(strided(h5, 0, count), o6[0:channels, :])
                          + dot(strided(h5, 1, count), o6[channels : 2 * channels, :])))

    def layer7():
        hidden = gelu(dot(strided(h6, 0, frames), o7[0:channels, :])
                      + dot(strided(h6, 1, frames), o7[channels : 2 * channels, :])).astype(jnp.float32)
        average = jnp.mean(hidden, axis=1, keepdims=True)
        away = hidden - average
        variance = jnp.mean(away * away, axis=1, keepdims=True)
        normed = away * lax.rsqrt(variance + 1e-05) * gain_ref[...] + shift_ref[...]
        store(h5, 0, normed)

    def project():
        normed = jnp.concatenate([h5[l, 0:frames, :] for l in range(channels // 128)], 1).astype(jnp.bfloat16)
        pieces = [
            lax.dot_general(normed, op[owner], (((1,), (1,)), ((), ())), preferred_element_type=jnp.float32)
            for owner in range(4)
        ]
        fr[...] = (jnp.concatenate(pieces, 1) + bias_ref[...]).astype(jnp.bfloat16)

    stages = (layer5, layer6, layer7, project)

    def finish(w):
        for slot in range(6):
            crossed[w, slot].wait_recv()
        loads[w].wait()
        stages[w]()

    for w in range(4):
        for slot in (4, 5):
            relayed[w, slot].wait_recv()
            pass_on(w, slot)
        if w >= 1:
            finish(w - 1)
    finish(3)
    for j in range(ITERS * CAP):
        rows_out = dot(picked[j].astype(jnp.bfloat16), fr[...])
        for l in range(6):
            laid[pl.ds(j * 6 + l, ranks, stride=PIECES), :] = rows_out[:, l * lanes : (l + 1) * lanes]

    @pl.loop(0, 8)
    def _(c):
        flat = laid[pl.ds(pl.multiple_of(c * lot * PIECES, lot * PIECES), lot * PIECES), :]
        sent[pl.ds(c * lot, lot)] = flat.reshape(lot, PIECES, 128).astype(jnp.bfloat16)

    @for_peers
    def _(peer):
        pltpu.make_async_remote_copy(
            src_ref=sent.at[peer], dst_ref=got.at[rec], send_sem=go_sem, recv_sem=come_sem.at[level],
            device_id=(peer, grp), device_id_type=MESH,
        ).start()

    own = pltpu.make_async_copy(sent.at[rec], got.at[rec], own_sem)
    own.start()
    own.wait()
    every = pltpu.make_async_remote_copy(
        src_ref=sent.at[pl.ds(0, ranks - 1)], dst_ref=got.at[pl.ds(0, ranks - 1)], send_sem=go_sem,
        recv_sem=come_sem.at[0], device_id=mate, device_id_type=MESH,
    )

    def arrived(c, count):
        pltpu.make_async_remote_copy(
            src_ref=sent.at[pl.ds(0, count)], dst_ref=got.at[pl.ds(0, count)], send_sem=go_sem,
            recv_sem=come_sem.at[c], device_id=mate, device_id_type=MESH,
        ).wait_recv()

    shape = (lot, PIECES, 128)
    piece = lax.broadcasted_iota(jnp.int32, shape, 1)
    lane = lax.broadcasted_iota(jnp.int32, shape, 2)
    in_row = lane == piece // 6
    column = (lot, PIECES, 1)
    piece_column = lax.broadcasted_iota(jnp.int32, column, 1)
    base = ((piece_column // 12) * 6 + lax.rem(piece_column, 6)) * 8 - 1
    wide_lane = lax.broadcasted_iota(jnp.int32, (lot, PIECES, 256), 2)
    contract = (((0,), (0,)), ((), ()))
    ones = jnp.ones((lot * PIECES, 128), jnp.bfloat16)

    def add_up(c, carry):
        sums, hits = carry
        block = got[pl.ds(c * lot, lot)].astype(jnp.float32)
        meta = jnp.broadcast_to(block[:, 36:37, :], shape)
        tag = jnp.sum(jnp.where(in_row, meta, 0.0), axis=2, keepdims=True).astype(jnp.int32)
        spot = jnp.where(tag == 0, -1, base + jnp.abs(tag))
        hot = jnp.where(wide_lane == spot, 1.0, 0.0)
        live = jnp.where(tag > 0, hot, 0.0)
        onehot[pl.ds(pl.multiple_of(c * lot * PIECES, lot * PIECES), lot * PIECES), :] = (
            hot.reshape(lot * PIECES, 256).astype(jnp.bfloat16)
        )
        live = live.reshape(lot * PIECES, 256).astype(jnp.bfloat16)
        flat = block.reshape(lot * PIECES, 128).astype(jnp.bfloat16)
        sums = sums + lax.dot_general(live, flat, contract, preferred_element_type=jnp.float32)
        hits = hits + lax.dot_general(live, ones, contract, preferred_element_type=jnp.float32)
        return sums, hits

    zero = jnp.zeros((256, 128), jnp.float32)
    def next_level(i, carry):
        c = lax.rem(level + i, 8)
        arrived(c, lot)
        return add_up(c, carry)

    arrived(level, lot - 1)
    sums, hits = lax.fori_loop(1, 8, next_level, add_up(level, (zero, zero)))
    part[0:144, :] = sums[0:144]
    for t in range(ITERS):
        part[144 + 8 * t : 152 + 8 * t, :] = hits[48 * t : 48 * t + 8]

    copies = []
    for step in (2, 1, 3):
        made = pltpu.make_async_remote_copy(
            src_ref=part, dst_ref=held.at[grp], send_sem=part_send.at[step - 1],
            recv_sem=part_come.at[step - 1], device_id=(rec, lax.rem(grp + step, 4)), device_id_type=MESH,
        )
        made.start()
        copies.append(made)
    held[grp] = part[...]
    for made in copies:
        made.wait()

    code[144:256, :] = jnp.zeros((112, 128), jnp.float32)
    for l in range(6):
        centroid = start_ref[:, l * lanes : (l + 1) * lanes]
        counts = prior_ref[...]
        for t in range(ITERS):
            at = (t * 6 + l) * 8
            code[at : at + 8, :] = centroid.astype(jnp.bfloat16).astype(jnp.float32)
            total = (held[0, at : at + 8] + held[1, at : at + 8]) + (
                held[2, at : at + 8] + held[3, at : at + 8]
            )
            at = 144 + 8 * t
            more = (held[0, at : at + 8] + held[1, at : at + 8]) + (
                held[2, at : at + 8] + held[3, at : at + 8]
            )
            updated = counts + more
            centroid = (counts * centroid + total) / updated
            counts = updated
        centroid_out[:, l * lanes : (l + 1) * lanes] = centroid
    table = code[...].astype(jnp.bfloat16)

    @pl.loop(0, 8)
    def _(c):
        block = got[pl.ds(c * lot, lot)].astype(jnp.float32)
        hot = onehot[pl.ds(pl.multiple_of(c * lot * PIECES, lot * PIECES), lot * PIECES), :]
        named = jnp.dot(hot, table, preferred_element_type=jnp.float32).reshape(shape)
        gap = block - named
        apart = jnp.sum(gap * gap, axis=2, keepdims=True)
        spread = jnp.where(in_row, apart, 0.0)
        reply[pl.ds(c * lot, lot)] = jnp.sum(spread, axis=1, keepdims=True) / width

    @for_peers
    def _(peer):
        pltpu.make_async_remote_copy(
            src_ref=reply.at[peer], dst_ref=back.at[rec], send_sem=reply_send, recv_sem=reply_come,
            device_id=(peer, grp), device_id_type=MESH,
        ).start()

    own = pltpu.make_async_copy(reply.at[rec], back.at[rec], own_sem)
    own.start()
    own.wait()
    all_back = pltpu.make_async_remote_copy(
        src_ref=reply.at[pl.ds(0, ranks - 1)], dst_ref=back.at[pl.ds(0, ranks - 1)], send_sem=reply_send,
        recv_sem=reply_come, device_id=mate, device_id_type=MESH,
    )
    all_back.wait_recv()
    replies = back[...].reshape(ranks, 128)
    for t in range(ITERS):
        one = jnp.zeros((1, frames), jnp.float32)
        for s in range(CAP):
            j = t * CAP + s
            one = one + jnp.sum(picked[j] * replies[:, j : j + 1], axis=0, keepdims=True)
        dist_out[t] = one
    next_rows.wait_send()
    for w in range(4):
        for slot in range(6):
            crossed[w, slot].wait_send()
        for made in [direct[w, slot] for slot in range(4)] + [relayed[w, slot] for slot in (4, 5)]:
            made.wait_send()
    every.wait_send()
    all_back.wait_send()


def shards(
    conv_in,
    conv5_weight,
    conv6_weight,
    conv7_weight,
    norm_gain,
    norm_bias,
    proj_weight,
    proj_bias,
    rec_length,
    assign,
    centroid_init,
    prior_count,
):
    ranks = lax.axis_size("rec")
    signal = conv_in[0]
    steps, channels = signal.shape
    frames = steps // 8
    slots, width = centroid_init.shape
    prior = jnp.broadcast_to(prior_count[:, None], (slots, 128))
    vmem = pl.BlockSpec(memory_space=pltpu.VMEM)
    hbm = pl.BlockSpec(memory_space=pltpu.HBM)
    smem = pl.BlockSpec(memory_space=pltpu.SMEM)
    bf16, f32, dma = jnp.bfloat16, jnp.float32, pltpu.SemaphoreType.DMA
    return pl.pallas_call(
        whole_kernel,
        out_shape=[
            jax.ShapeDtypeStruct(assign.shape, f32),
            jax.ShapeDtypeStruct(centroid_init.shape, f32),
        ],
        in_specs=[hbm] * 5 + [vmem] * 3 + [smem] + [vmem] * 3,
        out_specs=[vmem] * 2,
        scratch_shapes=[
            pltpu.VMEM((3 * channels, channels), bf16),
            pltpu.VMEM((2 * channels, channels), bf16),
            pltpu.VMEM((2 * channels, channels), bf16),
            pltpu.VMEM((4,) + proj_weight.shape[::-1], bf16),
            pltpu.VMEM((16, channels), bf16),
            pltpu.VMEM((steps, channels), bf16),
            pltpu.VMEM((channels // 128, steps + 8, 128), f32),
            pltpu.VMEM((channels // 128, steps // 2, 128), f32),
            pltpu.VMEM((channels // 128, steps // 4, 128), f32),
            pltpu.VMEM((frames, width), bf16),
            pltpu.VMEM((ITERS * CAP, ranks, frames), f32),
            pltpu.VMEM((ranks * PIECES, 128), f32),
            pltpu.VMEM((ranks, PIECES, 128), bf16),
            pltpu.VMEM((ranks, PIECES, 128), bf16),
            pltpu.VMEM((ranks * PIECES, 256), bf16),
            pltpu.VMEM((168, 128), f32),
            pltpu.VMEM((4, 168, 128), f32),
            pltpu.VMEM((256, 128), f32),
            pltpu.VMEM((ranks, 1, 128), f32),
            pltpu.VMEM((ranks, 1, 128), f32),
            dma((4, 12)), dma((4, 6)), dma((4, 6)), dma((5,)), dma, dma,
            dma, dma((8,)), dma, dma((3,)), dma((3,)), dma, dma,
        ],
        compiler_params=pltpu.CompilerParams(
            collective_id=0, has_side_effects=True, vmem_limit_bytes=63 * 1024 * 1024
        ),
    )(
        signal, conv5_weight, conv6_weight, conv7_weight, proj_weight.T, norm_gain[None], norm_bias[None],
        proj_bias[None], rec_length, assign, centroid_init, prior,
    )


def solution(mesh):
    in_specs = (
        P("grp", "rec", None),
        P(None, "grp"),
        P(None, "grp"),
        P(None, "grp"),
        P(),
        P(),
        P(None, "grp"),
        P(),
        P("grp"),
        P(None, "grp", "rec"),
        P("rec", None),
        P("rec"),
    )
    out_specs = (P(None, "grp", "rec"), P("rec", None))
    return jax.shard_map(shards, mesh=mesh, in_specs=in_specs, out_specs=out_specs, check_vma=False)
```
